512 devices in a mesh: dp: 32 (over y, x, core), tensor: 16 (over z).
Axes of the slice: x: 4, y: 4, z: 16, core: 2. Of those that a mesh axis runs over, the one named last changes fastest.
Arguments:
- tokens: bfloat16 [14336, 8192], P('dp', 'tensor'), may hold values from -6 to 6
- weight: bfloat16 [8192, 2048], P('tensor'), may hold values from -0.09375 to 0.09375
- cotangent: bfloat16 [14336, 2048], P('dp', 'tensor'), may hold values from -6 to 6
- slot_job: int32 [448], replicated, may hold values from 0 to 447, as said below
- slot_count: int32 [448], P('dp'), may hold values from 1 to 32
- adapter_down: float32 [448, 8, 8192], P('dp', None, 'tensor'), may hold values from -0.0625 to 0.0625
- adapter_up: float32 [448, 8, 2048], P('dp', None, 'tensor'), may hold values from -1 to 1
- down_first: float32 [448, 8, 8192], P('dp', None, 'tensor'), may hold values from -4 to 4
- down_second: float32 [448, 8, 8192], P('dp', None, 'tensor'), may hold values from 0.01 to 1
- up_first: float32 [448, 8, 2048], P('dp', None, 'tensor'), may hold values from -4 to 4
- up_second: float32 [448, 8, 2048], P('dp', None, 'tensor'), may hold values from 0.01 to 1
Outputs:
- values: bfloat16 [14336, 2048], P('dp', 'tensor')
- token_grad: bfloat16 [14336, 8192], P('dp', 'tensor')
- new_down: float32 [448, 8, 8192], P('dp', None, 'tensor')
- new_down_first: float32 [448, 8, 8192], P('dp', None, 'tensor')
- new_down_second: float32 [448, 8, 8192], P('dp', None, 'tensor')
- new_up: float32 [448, 8, 2048], P('dp', None, 'tensor')
- new_up_first: float32 [448, 8, 2048], P('dp', None, 'tensor')
- new_up_second: float32 [448, 8, 2048], P('dp', None, 'tensor')
The draws below stay inside these ranges and needn't reach their ends.
Inputs may be any that keep to these rules, and one draw needn't show every extreme that they name: `slot_job`: every job stands in exactly one slot. Slots 14 * g to 14 * g + 13 form token group g. The adapters and moments of job j are stored at dp index j // 14, and no group holds two jobs whose adapters are stored at the same dp index.
All inputs are finite; a program needn't handle non-finite values.
Results may differ from the reference program's by a relative error of at most 0.0028.
Values may be sent and summed in bfloat16 or wider, within the bound.
A program may use at most 64 MiB of HBM per device.

```python
import math
import jax
import jax.numpy as jnp
from jax import lax

D = 8192
KV = 2048
RANK = 8
BLOCK = 32
SLOTS = 14
JOBS = 448
TOKENS = 14336


def draw_slot_job(key, part):
    group_count = JOBS // SLOTS
    key_list = jax.random.split(key, 5)
    offsets = jax.random.permutation(key_list[0], group_count)[:SLOTS].astype(jnp.int32)
    owner_perm = jax.random.permutation(key_list[1], group_count).astype(jnp.int32)
    group_perm = jax.random.permutation(key_list[2], group_count).astype(jnp.int32)
    local_perm = jax.vmap(lambda sub_key: jax.random.permutation(sub_key, SLOTS))(jax.random.split(key_list[3], group_count)).astype(jnp.int32)
    slot_perm = jax.vmap(lambda sub_key: jax.random.permutation(sub_key, SLOTS))(jax.random.split(key_list[4], group_count)).astype(jnp.int32)
    row_idx = jnp.arange(group_count, dtype=jnp.int32)[:, None]
    col_idx = jnp.arange(SLOTS, dtype=jnp.int32)[None, :]
    source = (row_idx - offsets[None, :]) % group_count
    owner = owner_perm[source]
    job_ids = owner * SLOTS + local_perm[owner, col_idx]
    position = group_perm[row_idx] * SLOTS + slot_perm[row_idx, col_idx]
    result = jnp.zeros((JOBS,), jnp.int32).at[position.reshape(-1)].set(job_ids.reshape(-1).astype(jnp.int32))
    return result


def set_ends(values, key, smallest, high):
    spot = [jax.random.randint(jax.random.fold_in(key, axis), (), 0, length) for axis, length in enumerate(values.shape)]
    main_axis = values.shape.index(max(values.shape))
    beside = spot[:main_axis] + [(spot[main_axis] + 1) % values.shape[main_axis]] + spot[main_axis + 1:]
    return values.at[tuple(spot)].set(smallest).at[tuple(beside)].set(high)


def strengthened(drawn, own_key, source, target, shards_of, factor):
    owner, partner = [(jnp.arange(drawn.shape[dim]) // (drawn.shape[dim] // shards_of)).reshape([-1 if axis == dim else 1 for axis in range(drawn.ndim)]) for dim in (source, target)]
    chosen = jax.random.permutation(own_key, shards_of)[partner]
    strong = (owner == chosen) | (owner == (partner + shards_of // 2) % shards_of)
    return jnp.where(strong, factor * drawn, drawn)


def level_of(own_key, extent, cuts, low, high):
    loudness = 1.0
    for axis_at, shards_of in cuts:
        draws = jax.random.uniform(jax.random.fold_in(jax.random.fold_in(own_key, 6), axis_at), (shards_of,), jnp.float32, low / len(cuts), high / len(cuts))
        loudness = loudness * jnp.repeat(jnp.exp(draws), extent[axis_at] // shards_of).reshape((-1,) + (1,) * (len(extent) - 1 - axis_at))
    return loudness


def bell_draw(key, extent, scale, reach, cuts=(), held_as=jnp.bfloat16):
    entries = jax.random.normal(key, extent, jnp.float32) * scale
    if len(cuts) > 0:
        entries = level_of(key, extent, cuts, -0.22, 0.18) * entries
    return jnp.clip(entries, min=-reach, max=reach).astype(held_as)


def gaussian_with(stream_key, extent, scale, reach, pieces, heavy, held_as=jnp.bfloat16):
    values = scale * jax.random.normal(stream_key, extent, jnp.float32)
    if pieces:
        values = values * level_of(stream_key, extent, pieces, -0.22, 0.18)
    return jnp.clip(strengthened(values, jax.random.fold_in(stream_key, 3), *heavy), -reach, reach).astype(held_as)


def setup_inputs(seed: int = 0) -> dict:
    key_of = jax.random.split(jax.random.key(seed), 12)
    return {
        "tokens": bell_draw(key_of[0], (TOKENS, D), 1.0, 6.0, ((0, 32), (1, 16))),
        "weight": gaussian_with(key_of[1], (D, KV), D ** -0.5, 0.09375, ((0, 16),), (0, 1, 16, 2.0)),
        "cotangent": bell_draw(key_of[2], (TOKENS, KV), 1.0, 6.0, ((0, 32), (1, 16))),
        "slot_job": draw_slot_job(jax.random.fold_in(key_of[11], 71), 0),
        "slot_count": set_ends(jax.random.randint(key_of[4], (JOBS,), 1, BLOCK + 1), jax.random.fold_in(key_of[4], 1), 1, BLOCK).astype(jnp.int32),
        "adapter_down": bell_draw(key_of[5], (JOBS, RANK, D), D ** -0.5, 0.0625, ((0, 32), (2, 16)), jnp.float32),
        "adapter_up": bell_draw(key_of[6], (JOBS, RANK, KV), 0.0625, 1.0, ((0, 32), (2, 16)), jnp.float32),
        "down_first": bell_draw(key_of[7], (JOBS, RANK, D), 0.3, 4.0, ((0, 32), (2, 16)), jnp.float32),
        "down_second": jnp.clip(jnp.exp(math.log(1.0) - 4.6051702 * jax.random.uniform(key_of[8], (JOBS, RANK, D), jnp.float32) ** level_of(key_of[8], (JOBS, RANK, D), ((0, 32), (2, 16)), -0.2, 0.2)), 0.01, 1.0),
        "up_first": bell_draw(key_of[9], (JOBS, RANK, KV), 0.3, 4.0, ((0, 32), (2, 16)), jnp.float32),
        "up_second": jnp.clip(jnp.exp(math.log(1.0) - 4.6051702 * jax.random.uniform(key_of[10], (JOBS, RANK, KV), jnp.float32) ** level_of(key_of[10], (JOBS, RANK, KV), ((0, 32), (2, 16)), -0.2, 0.2)), 0.01, 1.0),
    }


lowrank_scale = 2.0
learn_rate = 0.001
beta_first = 0.9
beta_second = 0.999
adam_eps = 1e-08
adam_step = 20.0

def adam_update(param, first, second, grad):
    new_first = beta_first * first + (1.0 - beta_first) * grad
    new_second = beta_second * second + (1.0 - beta_second) * grad * grad
    fix_first = 1.0 - beta_first ** adam_step
    fix_second = 1.0 - beta_second ** adam_step
    new_param = param - learn_rate * (new_first / fix_first) / (jnp.sqrt(new_second / fix_second) + adam_eps)
    return (new_param, new_first, new_second)

def reference(tokens, weight, cotangent, slot_job, slot_count, adapter_down, adapter_up, down_first, down_second, up_first, up_second):
    highest = lax.Precision.HIGHEST
    down_slot = adapter_down.astype(jnp.bfloat16)[slot_job].astype(jnp.float32)
    up_slot = adapter_up.astype(jnp.bfloat16)[slot_job].astype(jnp.float32)
    tok_blocks = tokens.reshape(JOBS, BLOCK, D).astype(jnp.float32)
    low_rank = jnp.einsum('bpd,brd->bpr', tok_blocks, down_slot, precision=highest)
    base = jnp.dot(tokens, weight, preferred_element_type=jnp.float32)
    branch = jnp.einsum('bpr,brk->bpk', low_rank, up_slot, precision=highest).reshape(TOKENS, KV)
    values = (base + lowrank_scale * branch).astype(jnp.bfloat16)
    positions = jnp.arange(BLOCK, dtype=jnp.int32)
    live_mask = (positions[None, :] < slot_count[:, None]).astype(jnp.bfloat16)
    masked_cot = cotangent.reshape(JOBS, BLOCK, KV) * live_mask[:, :, None]
    cot_float = masked_cot.astype(jnp.float32)
    up_rank = jnp.einsum('bpk,brk->bpr', cot_float, up_slot, precision=highest)
    back_base = jnp.dot(masked_cot.reshape(TOKENS, KV), weight.T, preferred_element_type=jnp.float32)
    back_branch = jnp.einsum('bpr,brd->bpd', up_rank, down_slot, precision=highest).reshape(TOKENS, D)
    token_grad = (back_base + lowrank_scale * back_branch).astype(jnp.bfloat16)
    factor = lowrank_scale / slot_count.astype(jnp.float32)
    grad_down_slot = factor[:, None, None] * jnp.einsum('bpr,bpd->brd', up_rank, tok_blocks, precision=highest)
    grad_up_slot = factor[:, None, None] * jnp.einsum('bpr,bpk->brk', low_rank, cot_float, precision=highest)
    grad_down = jnp.zeros((JOBS, RANK, D), jnp.float32).at[slot_job].set(grad_down_slot)
    grad_up = jnp.zeros((JOBS, RANK, KV), jnp.float32).at[slot_job].set(grad_up_slot)
    new_down, new_down_first, new_down_second = adam_update(adapter_down, down_first, down_second, grad_down)
    new_up, new_up_first, new_up_second = adam_update(adapter_up, up_first, up_second, grad_up)
    return (values, token_grad, new_down, new_down_first, new_down_second, new_up, new_up_first, new_up_second)
```

```python
import functools

import jax
import jax.numpy as jnp
from jax import lax
from jax.experimental import pallas as pl
from jax.experimental.pallas import tpu as pltpu
from jax.sharding import PartitionSpec as P

lowrank_scale = 2.0
learn_rate = 0.001
beta_first = 0.9
beta_second = 0.999
adam_eps = 1e-08
adam_step = 20.0
small_lag = 2
sum_lag = 5
MESH = pl.DeviceIdType.MESH


def adam_update(param, first, second, grad):
    new_first = beta_first * first + (1.0 - beta_first) * grad
    new_second = beta_second * second + (1.0 - beta_second) * grad * grad
    fix_first = 1.0 - beta_first**adam_step
    fix_second = 1.0 - beta_second**adam_step
    new_param = param - learn_rate * (new_first / fix_first) / (
        jnp.sqrt(new_second / fix_second) + adam_eps
    )
    return (new_param, new_first, new_second)


def dot(a, b, dims):
    return lax.dot_general(a, b, (dims, ((), ())), preferred_element_type=jnp.float32)


def dot_split(a, b, dims):
    high = a.astype(jnp.bfloat16)
    rest = (a - high.astype(jnp.float32)).astype(jnp.bfloat16)
    return dot(high, b, dims) + dot(rest, b, dims)


def step_kernel(
    n_dp,
    n_z,
    route_ref,
    count_ref,
    factor_ref,
    tok_ref,
    w_ref,
    cot_ref,
    ad_ref,
    au_ref,
    df_ref,
    ds_ref,
    uf_ref,
    us_ref,
    val_ref,
    tg_ref,
    nd_ref,
    ndf_ref,
    nds_ref,
    nu_ref,
    nuf_ref,
    nus_ref,
    send_a,
    recv_a,
    send_g,
    recv_g,
    slot_a,
    slot_g,
    ag,
    sm,
    part,
    out_r,
    in_r,
    out_l,
    in_l,
    back,
    sem_as,
    sem_ar,
    sem_gs,
    sem_gr,
    ag_rs,
    ag_rr,
    ag_ls,
    ag_lr,
    sm_rs,
    sm_rr,
    sm_ls,
    sm_lr,
    rs_rs,
    rs_rr,
    rs_ls,
    rs_lr,
):
    my_dp = lax.axis_index("dp")
    me = lax.axis_index("tensor")
    right = lax.rem(me + 1, n_z)
    left = lax.rem(me + n_z - 1, n_z)
    n_right = n_z // 2
    n_left = n_z - 1 - n_right
    slots, rank, width = ad_ref.shape
    cols = cot_ref.shape[1]
    rows = tok_ref.shape[0]
    block = rows // slots

    barrier = pltpu.get_barrier_semaphore()
    pl.semaphore_signal(barrier, inc=1, device_id={"tensor": right}, device_id_type=MESH)
    pl.semaphore_signal(barrier, inc=1, device_id={"tensor": left}, device_id_type=MESH)

    def greet(i, carry):
        other = lax.rem(my_dp + i, n_dp)
        pl.semaphore_signal(barrier, inc=1, device_id={"dp": other}, device_id_type=MESH)
        return carry

    lax.fori_loop(1, n_dp, greet, 0)

    def pack(g, carry):
        j = route_ref[0, g]
        send_a[g, :, :width] = ad_ref[j].astype(jnp.bfloat16)
        send_a[g, :, width:] = au_ref[j].astype(jnp.bfloat16)
        return carry

    lax.fori_loop(0, n_dp, pack, 0)
    at_row = lax.broadcasted_iota(jnp.int32, (block, cols), 0)
    for b in range(slots):
        here = pl.ds(b * block, block)
        ag[me, here, :] = jnp.where(
            at_row < count_ref[b], cot_ref[here, :].astype(jnp.float32), 0.0
        ).astype(jnp.bfloat16)

    pl.semaphore_wait(barrier, n_dp + 1)

    def adapter_copy(other, slot):
        return pltpu.make_async_remote_copy(
            src_ref=send_a.at[other],
            dst_ref=recv_a.at[slot],
            send_sem=sem_as.at[other],
            recv_sem=sem_ar.at[slot],
            device_id={"dp": other},
            device_id_type=MESH,
        )

    def grad_copy(other, slot):
        return pltpu.make_async_remote_copy(
            src_ref=send_g.at[other],
            dst_ref=recv_g.at[slot],
            send_sem=sem_gs.at[other],
            recv_sem=sem_gr.at[slot],
            device_id={"dp": other},
            device_id_type=MESH,
        )

    def every_other(action):
        def body(i, carry):
            action(lax.rem(my_dp + i, n_dp))
            return carry

        lax.fori_loop(1, n_dp, body, 0)

    def gather_copy(buf, sems, to_right, step):
        send_sem, recv_sem = sems
        owner = lax.rem(me + (n_z - step if to_right else step), n_z)
        return pltpu.make_async_remote_copy(
            src_ref=buf.at[owner],
            dst_ref=buf.at[owner],
            send_sem=send_sem.at[step],
            recv_sem=recv_sem.at[step],
            device_id={"tensor": right if to_right else left},
            device_id_type=MESH,
        )

    def gather_arrival(buf, sems, to_right, step):
        send_sem, recv_sem = sems
        owner = lax.rem(me + (2 * n_z - 1 - step if to_right else step + 1), n_z)
        pltpu.make_async_remote_copy(
            src_ref=buf.at[owner],
            dst_ref=buf.at[owner],
            send_sem=send_sem.at[step],
            recv_sem=recv_sem.at[step],
            device_id={"tensor": right if to_right else left},
            device_id_type=MESH,
        ).wait_recv()
        return owner

    def sum_copy(to_right, step):
        return pltpu.make_async_remote_copy(
            src_ref=(out_r if to_right else out_l).at[step],
            dst_ref=(in_r if to_right else in_l).at[step],
            send_sem=(rs_rs if to_right else rs_ls).at[step],
            recv_sem=(rs_rr if to_right else rs_lr).at[step],
            device_id={"tensor": right if to_right else left},
            device_id_type=MESH,
        )

    ag_right, ag_left = (ag_rs, ag_rr), (ag_ls, ag_lr)
    sm_right, sm_left = (sm_rs, sm_rr), (sm_ls, sm_lr)

    every_other(lambda other: adapter_copy(other, my_dp).start())
    gather_copy(ag, ag_right, True, 0).start()
    gather_copy(ag, ag_left, False, 0).start()
    recv_a[my_dp] = send_a[my_dp]

    def columns(c):
        return pl.ds(pl.multiple_of(c * cols, cols), cols)

    def forward(c, carry):
        part[c] = dot(tok_ref[...], w_ref[:, columns(c)], ((1,), (0,)))
        return carry

    lax.fori_loop(0, n_z, forward, 0)

    def backward(c, first=False):
        term = dot(ag[c], w_ref[:, columns(c)], ((1,), (1,)))
        back[...] = term if first else back[...] + term

    backward(me, True)

    of_slot = lax.broadcasted_iota(jnp.int32, (slots, rank, rows), 2) // block
    own_slot = of_slot == lax.broadcasted_iota(jnp.int32, (slots, rank, rows), 0)

    def fold(full):
        return jnp.sum(jnp.where(own_slot, full.reshape(slots, rank, rows), 0.0), axis=0)

    def unfold(ranks):
        return jnp.where(own_slot, ranks[None], 0.0).reshape(slots * rank, rows)

    def small_begin():
        every_other(lambda other: adapter_copy(my_dp, other).wait_recv())
        for b in range(slots):
            slot_a[b * rank : (b + 1) * rank, :] = recv_a[route_ref[1, b]].astype(jnp.float32)
        own = slot_a[...].astype(jnp.bfloat16)
        sm[me, :rank, :] = fold(dot(own[:, :width], tok_ref[...], ((1,), (1,))))
        sm[me, rank:, :] = fold(dot(own[:, width:], ag[me], ((1,), (1,))))
        gather_copy(sm, sm_right, True, 0).start()
        gather_copy(sm, sm_left, False, 0).start()

    def small_end():
        total = sm[0]
        for c in range(1, n_z):
            total = total + sm[c]
        low = unfold(total[:rank])
        up = unfold(total[rank:])
        grads = (
            dot_split(up, tok_ref[...], ((1,), (0,))),
            dot_split(low, ag[me], ((1,), (0,))),
        )
        for b in range(slots):
            for grad, at in zip(grads, (pl.ds(0, width), pl.ds(width, cols))):
                slot_g[b, :, at] = factor_ref[b] * grad[b * rank : (b + 1) * rank]

        def pack_grad(g, carry):
            send_g[g] = slot_g[route_ref[2, g]]
            return carry

        lax.fori_loop(0, n_dp, pack_grad, 0)
        every_other(lambda other: grad_copy(other, my_dp).start())
        recv_g[my_dp] = send_g[my_dp]
        own = slot_a[...].astype(jnp.bfloat16)
        back[...] += lowrank_scale * dot_split(up, own[:, :width], ((0,), (0,)))
        part[me] += lowrank_scale * dot_split(low, own[:, width:], ((0,), (0,)))

    def update():
        every_other(lambda other: grad_copy(my_dp, other).wait_recv())

        def one(j, carry):
            grad = recv_g[route_ref[3, j]]
            nd_ref[j], ndf_ref[j], nds_ref[j] = adam_update(
                ad_ref[j], df_ref[j], ds_ref[j], grad[:, :width]
            )
            nu_ref[j], nuf_ref[j], nus_ref[j] = adam_update(
                au_ref[j], uf_ref[j], us_ref[j], grad[:, width:]
            )
            return carry

        lax.fori_loop(0, slots, one, 0)

    def sum_send(step):
        for to_right, out, arrived, last in (
            (True, out_r, in_r, n_right),
            (False, out_l, in_l, n_left),
        ):
            if step > last:
                continue
            if step > 0:
                sum_copy(to_right, step - 1).wait_recv()
            if step < last:
                ahead = last - step
                c = lax.rem(me + (ahead if to_right else n_z - ahead), n_z)
                term = part[c]
                if step > 0:
                    term = term + arrived[step - 1]
                out[step] = term
                sum_copy(to_right, step).start()

    for t in range(max(n_right + sum_lag + 1, n_right + small_lag + 2)):
        if t < n_right:
            for to_right, sems, last in ((True, ag_right, n_right), (False, ag_left, n_left)):
                if t < last:
                    owner = gather_arrival(ag, sems, to_right, t)
                    if t + 1 < last:
                        gather_copy(ag, sems, to_right, t + 1).start()
                    backward(owner)
        s = t - small_lag
        if s == 0:
            small_begin()
        if 0 < s <= n_right:
            for to_right, sems, last in ((True, sm_right, n_right), (False, sm_left, n_left)):
                if s - 1 < last:
                    gather_arrival(sm, sems, to_right, s - 1)
                    if s < last:
                        gather_copy(sm, sems, to_right, s).start()
        s = t - sum_lag
        if 0 <= s <= n_right:
            sum_send(s)
        if t - small_lag == n_right:
            small_end()
        if t == n_right + small_lag + 2:
            update()
    if n_right + small_lag + 2 >= max(n_right + sum_lag + 1, n_right + small_lag + 2):
        update()

    tg_ref[...] = back[...].astype(jnp.bfloat16)
    val_ref[...] = (part[me] + in_r[n_right - 1] + in_l[n_left - 1]).astype(jnp.bfloat16)

    every_other(lambda other: adapter_copy(other, my_dp).wait_send())
    every_other(lambda other: grad_copy(other, my_dp).wait_send())
    for to_right, last in ((True, n_right), (False, n_left)):
        for step in range(last):
            gather_copy(ag, ag_right if to_right else ag_left, to_right, step).wait_send()
            gather_copy(sm, sm_right if to_right else sm_left, to_right, step).wait_send()
            sum_copy(to_right, step).wait_send()


def per_device(
    tokens,
    weight,
    cotangent,
    slot_job,
    slot_count,
    adapter_down,
    adapter_up,
    down_first,
    down_second,
    up_first,
    up_second,
):
    n_dp = lax.axis_size("dp")
    n_z = lax.axis_size("tensor")
    slots, rank, width = adapter_down.shape
    cols = adapter_up.shape[2]
    rows = tokens.shape[0]
    group = lax.axis_index("dp")
    groups = jnp.arange(n_dp, dtype=jnp.int32)
    local = jnp.arange(slots, dtype=jnp.int32)
    my_jobs = lax.dynamic_slice_in_dim(slot_job, group * slots, slots)
    owner = my_jobs // slots
    job_group = slot_job.reshape(n_dp, slots)
    match = job_group[:, :, None] == (group * slots + local)[None, None, :]
    here = jnp.any(match, axis=1)
    job_for_group = jnp.sum(jnp.where(here, local[None, :], 0), axis=1)
    group_of_job = jnp.sum(jnp.where(here, groups[:, None], 0), axis=0)
    slot_for_owner = jnp.sum(
        jnp.where(owner[None, :] == groups[:, None], local[None, :], 0), axis=1
    )
    pad = (0, n_dp - slots)
    route = jnp.stack(
        [job_for_group, jnp.pad(owner, pad), slot_for_owner, jnp.pad(group_of_job, pad)]
    ).astype(jnp.int32)
    factor = lowrank_scale / slot_count.astype(jnp.float32)

    smem = pl.BlockSpec(memory_space=pltpu.SMEM)
    vmem = pl.BlockSpec(memory_space=pltpu.VMEM)
    n_right = n_z // 2
    n_left = n_z - 1 - n_right
    f32, bf16 = jnp.float32, jnp.bfloat16
    dma = pltpu.SemaphoreType.DMA
    down = jax.ShapeDtypeStruct(adapter_down.shape, f32)
    up = jax.ShapeDtypeStruct(adapter_up.shape, f32)
    ring_sems = [dma((n_right,)), dma((n_right,)), dma((n_left,)), dma((n_left,))]
    return pl.pallas_call(
        functools.partial(step_kernel, n_dp, n_z),
        out_shape=(
            jax.ShapeDtypeStruct(cotangent.shape, bf16),
            jax.ShapeDtypeStruct(tokens.shape, bf16),
            down,
            down,
            down,
            up,
            up,
            up,
        ),
        in_specs=[smem] * 3 + [vmem] * 9,
        out_specs=(vmem,) * 8,
        scratch_shapes=[
            pltpu.VMEM((n_dp, rank, width + cols), bf16),
            pltpu.VMEM((n_dp, rank, width + cols), bf16),
            pltpu.VMEM((n_dp, rank, width + cols), f32),
            pltpu.VMEM((n_dp, rank, width + cols), f32),
            pltpu.VMEM((slots * rank, width + cols), f32),
            pltpu.VMEM((slots, rank, width + cols), f32),
            pltpu.VMEM((n_z, rows, cols), bf16),
            pltpu.VMEM((n_z, 2 * rank, rows), f32),
            pltpu.VMEM((n_z, rows, cols), f32),
            pltpu.VMEM((n_right, rows, cols), f32),
            pltpu.VMEM((n_right, rows, cols), f32),
            pltpu.VMEM((n_left, rows, cols), f32),
            pltpu.VMEM((n_left, rows, cols), f32),
            pltpu.VMEM((rows, width), f32),
            dma((n_dp,)),
            dma((n_dp,)),
            dma((n_dp,)),
            dma((n_dp,)),
        ]
        + ring_sems * 3,
        compiler_params=pltpu.CompilerParams(collective_id=0, has_side_effects=True),
        name="adapter_step",
    )(
        route,
        slot_count,
        factor,
        tokens,
        weight,
        cotangent,
        adapter_down,
        adapter_up,
        down_first,
        down_second,
        up_first,
        up_second,
    )


def solution(mesh):
    in_specs = (
        P("dp", "tensor"),
        P("tensor", None),
        P("dp", "tensor"),
        P(),
        P("dp"),
        P("dp", None, "tensor"),
        P("dp", None, "tensor"),
        P("dp", None, "tensor"),
        P("dp", None, "tensor"),
        P("dp", None, "tensor"),
        P("dp", None, "tensor"),
    )
    out_specs = (
        P("dp", "tensor"),
        P("dp", "tensor"),
        P("dp", None, "tensor"),
        P("dp", None, "tensor"),
        P("dp", None, "tensor"),
        P("dp", None, "tensor"),
        P("dp", None, "tensor"),
        P("dp", None, "tensor"),
    )
    return jax.shard_map(
        per_device, mesh=mesh, in_specs=in_specs, out_specs=out_specs, check_vma=False
    )
```

```python
import functools

import jax
import jax.numpy as jnp
from jax import lax
from jax.experimental import pallas as pl
from jax.experimental.pallas import tpu as pltpu
from jax.sharding import PartitionSpec as P

lowrank_scale = 2.0
learn_rate = 0.001
beta_first = 0.9
beta_second = 0.999
adam_eps = 1e-08
adam_step = 20.0
small_lag = 1
sum_lag = 4
ln2 = 0.6931471805599453
inv_ln2 = 1.4426950408889634
code_bits = 14.0
code_rows = 16
MESH = pl.DeviceIdType.MESH


def adam_update(param, first, second, grad):
    new_first = beta_first * first + (1.0 - beta_first) * grad
    new_second = beta_second * second + (1.0 - beta_second) * grad * grad
    fix_first = 1.0 - beta_first**adam_step
    fix_second = 1.0 - beta_second**adam_step
    new_param = param - learn_rate * (new_first / fix_first) / (
        jnp.sqrt(new_second / fix_second) + adam_eps
    )
    return (new_param, new_first, new_second)


def dot(a, b, dims):
    return lax.dot_general(a, b, (dims, ((), ())), preferred_element_type=jnp.float32)


def dot_split(a, b, dims):
    high = a.astype(jnp.bfloat16)
    rest = (a - high.astype(jnp.float32)).astype(jnp.bfloat16)
    return dot(high, b, dims) + dot(rest, b, dims)


def encode(x, rows):
    top = jnp.max(jnp.abs(x), axis=0, keepdims=True)
    power = jnp.ceil(jnp.log(jnp.maximum(top, 1e-28)) * inv_ln2)
    fixed = jnp.round(x * jnp.exp((code_bits - power) * ln2)).astype(jnp.int32)
    tail = jnp.broadcast_to(power, (code_rows, x.shape[1])).astype(jnp.int32)
    return fixed.astype(jnp.int16), tail.astype(jnp.int16)


def decode(ref, rows):
    power = ref[rows:, :].astype(jnp.int32).astype(jnp.float32)[:1]
    return ref[:rows, :].astype(jnp.int32).astype(jnp.float32) * jnp.exp(
        (power - code_bits) * ln2
    )


def step_kernel(
    n_dp,
    n_z,
    job_ref,
    count_ref,
    to_group_ref,
    to_owner_ref,
    group_ref,
    tok_hbm,
    w_hbm,
    cot_ref,
    ad_ref,
    au_ref,
    val_ref,
    tg_ref,
    grad_ref,
    tok_ref,
    w_ref,
    send_a,
    recv_a,
    send_g,
    recv_g,
    slot_a,
    slot_g,
    ag,
    sm,
    part,
    sum_out,
    sum_in,
    back,
    load_sem,
    sem_as,
    sem_ar,
    sem_gs,
    sem_gr,
    ag_s,
    ag_r,
    sm_s,
    sm_r,
    rs_s,
    rs_r,
):
    my_dp = lax.axis_index("dp")
    me = lax.axis_index("tensor")
    right = lax.rem(me + 1, n_z)
    left = lax.rem(me + n_z - 1, n_z)
    hops = n_z // 2
    slots, rank, width = ad_ref.shape
    cols = cot_ref.shape[1]
    rows = cot_ref.shape[0]
    half = rows // 2
    block = rows // slots

    load_w = pltpu.make_async_copy(w_hbm, w_ref, load_sem.at[0])
    load_tok = pltpu.make_async_copy(tok_hbm, tok_ref, load_sem.at[1])
    load_tok.start()
    load_w.start()

    barrier = pltpu.get_barrier_semaphore()
    pl.semaphore_signal(barrier, inc=1, device_id={"tensor": right}, device_id_type=MESH)
    pl.semaphore_signal(barrier, inc=1, device_id={"tensor": left}, device_id_type=MESH)

    def greet(i, carry):
        other = lax.rem(my_dp + i, n_dp)
        pl.semaphore_signal(barrier, inc=1, device_id={"dp": other}, device_id_type=MESH)
        return carry

    lax.fori_loop(1, n_dp, greet, 0)

    at_row = lax.broadcasted_iota(jnp.int32, (block, cols), 0)
    for b in range(slots):
        here = pl.ds(b * block, block)
        ag[me, here, :] = jnp.where(
            at_row < count_ref[b], cot_ref[here, :].astype(jnp.float32), 0.0
        ).astype(jnp.bfloat16)

    def pack(g, carry):
        j = to_group_ref[g]
        send_a[g, :, :width] = ad_ref[j].astype(jnp.bfloat16)
        send_a[g, :, width:] = au_ref[j].astype(jnp.bfloat16)
        return carry

    lax.fori_loop(0, n_dp, pack, 0)
    pl.semaphore_wait(barrier, n_dp + 1)

    def adapter_copy(other, slot):
        return pltpu.make_async_remote_copy(
            src_ref=send_a.at[other],
            dst_ref=recv_a.at[slot],
            send_sem=sem_as.at[other],
            recv_sem=sem_ar.at[slot],
            device_id={"dp": other},
            device_id_type=MESH,
        )

    def grad_copy(other, slot):
        return pltpu.make_async_remote_copy(
            src_ref=send_g.at[other],
            dst_ref=recv_g.at[slot],
            send_sem=sem_gs.at[other],
            recv_sem=sem_gr.at[slot],
            device_id={"dp": other},
            device_id_type=MESH,
        )

    def every_other(action):
        def body(i, carry):
            action(lax.rem(my_dp + i, n_dp))
            return carry

        lax.fori_loop(1, n_dp, body, 0)

    streams = [(0, True), (1, False), (0, False), (1, True)]

    def length(stream):
        h, to_right = stream
        return hops if (h == 0) == to_right else hops - 1

    def index(stream):
        return stream[0] * 2 + int(stream[1])

    def ring_copy(buf, size, sems, stream, step, arriving):
        h, to_right = stream
        back_by = step + 1 if arriving else step
        owner = lax.rem(me + (2 * n_z - back_by if to_right else back_by), n_z)
        place = buf.at[owner, pl.ds(h * size, size), :]
        return pltpu.make_async_remote_copy(
            src_ref=place,
            dst_ref=place,
            send_sem=sems[0].at[index(stream), step],
            recv_sem=sems[1].at[index(stream), step],
            device_id={"tensor": right if to_right else left},
            device_id_type=MESH,
        )

    def gather(step, stream, arriving=False):
        return ring_copy(ag, half, (ag_s, ag_r), stream, step, arriving)

    def small(step, stream, arriving=False):
        return ring_copy(sm, rank, (sm_s, sm_r), stream, step, arriving)

    def relay(ring, step):
        for stream in streams:
            if step < length(stream):
                ring(step, stream, True).wait_recv()
                if step + 1 < length(stream):
                    ring(step + 1, stream).start()

    def sum_copy(step, stream):
        i = index(stream)
        return pltpu.make_async_remote_copy(
            src_ref=sum_out.at[i, step],
            dst_ref=sum_in.at[i, step],
            send_sem=rs_s.at[i, step],
            recv_sem=rs_r.at[i, step],
            device_id={"tensor": right if stream[1] else left},
            device_id_type=MESH,
        )

    def columns(c):
        return pl.ds(pl.multiple_of(c * cols, cols), cols)

    def chunk(offset):
        return lax.rem(me + n_z + offset, n_z)

    def forward(offsets):
        w = [w_ref[:, columns(chunk(o))] for o in offsets]
        w = w[0] if len(w) == 1 else jnp.concatenate(w, axis=1)
        product = dot(tok_ref[...], w, ((1,), (0,)))
        for i, o in enumerate(offsets):
            part[chunk(o)] = product[:, i * cols : (i + 1) * cols]

    def forward_for(step):
        ahead = hops - step
        forward([ahead, -ahead] if 0 < ahead < hops else [ahead])

    def backward(offsets, first=False):
        cot = [ag[chunk(o)] for o in offsets]
        w = [w_ref[:, columns(chunk(o))] for o in offsets]
        cot = cot[0] if len(cot) == 1 else jnp.concatenate(cot, axis=1)
        w = w[0] if len(w) == 1 else jnp.concatenate(w, axis=1)
        term = dot(cot, w, ((1,), (1,)))
        back[...] = term if first else back[...] + term

    def sum_step(step):
        for stream in streams:
            start = hops - length(stream)
            if step < start:
                continue
            h, to_right = stream
            i = index(stream)
            here = pl.ds(h * half, half)
            ahead = hops - step
            c = chunk(ahead if to_right else -ahead)
            total = part[c, here, :]
            if step > start:
                sum_copy(step - 1, stream).wait_recv()
                total = total + decode(sum_in.at[i, step - 1], half)
            if step == hops:
                part[c, here, :] = total
                continue
            sum_out[i, step, :half, :], sum_out[i, step, half:, :] = encode(total, half)
            sum_copy(step, stream).start()

    of_slot = lax.broadcasted_iota(jnp.int32, (slots, rank, rows), 2) // block
    own_slot = of_slot == lax.broadcasted_iota(jnp.int32, (slots, rank, rows), 0)

    def fold(full):
        return jnp.sum(jnp.where(own_slot, full.reshape(slots, rank, rows), 0.0), axis=0)

    def unfold(ranks):
        return jnp.where(own_slot, ranks[None], 0.0).reshape(slots * rank, rows)

    def small_begin():
        every_other(lambda other: adapter_copy(my_dp, other).wait_recv())
        for b in range(slots):
            owner = job_ref[my_dp * slots + b] // slots
            slot_a[b * rank : (b + 1) * rank, :] = recv_a[owner].astype(jnp.float32)
        own = slot_a[...].astype(jnp.bfloat16)
        sm[me, :rank, :] = fold(dot(own[:, :width], tok_ref[...], ((1,), (1,))))
        sm[me, rank:, :] = fold(dot(own[:, width:], ag[me], ((1,), (1,))))
        for stream in streams:
            small(0, stream).start()

    def small_end():
        total = sm[0]
        for c in range(1, n_z):
            total = total + sm[c]
        low = unfold(total[:rank])
        up = unfold(total[rank:])
        grads = (
            dot_split(up, tok_ref[...], ((1,), (0,))),
            dot_split(low, ag[me], ((1,), (0,))),
        )
        for b in range(slots):
            count = jnp.full((rank, cols), count_ref[b], jnp.int32).astype(jnp.float32)
            factor = (lowrank_scale / count)[:, :1]
            for grad, at in zip(grads, (pl.ds(0, width), pl.ds(width, cols))):
                slot_g[b, :, at] = factor * grad[b * rank : (b + 1) * rank]

        def pack_grad(g, carry):
            send_g[g] = slot_g[to_owner_ref[g]]
            return carry

        lax.fori_loop(0, n_dp, pack_grad, 0)
        every_other(lambda other: grad_copy(other, my_dp).start())
        recv_g[my_dp] = send_g[my_dp]
        return low, up

    def low_rank_terms(low, up):
        own = slot_a[...].astype(jnp.bfloat16)
        back[...] += lowrank_scale * dot_split(up, own[:, :width], ((0,), (0,)))
        part[me] += lowrank_scale * dot_split(low, own[:, width:], ((0,), (0,)))

    for stream in streams:
        gather(0, stream).start()
    every_other(lambda other: adapter_copy(other, my_dp).start())
    recv_a[my_dp] = send_a[my_dp]
    load_tok.wait()
    load_w.wait()
    forward_for(0)
    backward([0], True)

    for t in range(max(hops + sum_lag, hops + small_lag) + 1):
        s = t - small_lag
        if 0 < s <= hops:
            relay(small, s - 1)
        if t < hops:
            relay(gather, t)
        u = t - sum_lag
        if 0 <= u <= hops:
            sum_step(u)
        if s == 0:
            small_begin()
        if s == hops:
            low, up = small_end()
        if t < hops:
            backward([-1 - t, 1 + t] if t + 1 < hops else [hops])
        if t < hops:
            forward_for(t + 1)
        if s == hops:
            low_rank_terms(low, up)

    tg_ref[...] = back[...].astype(jnp.bfloat16)
    val_ref[...] = part[me].astype(jnp.bfloat16)
    every_other(lambda other: grad_copy(my_dp, other).wait_recv())

    def take(j, carry):
        grad_ref[j] = recv_g[group_ref[j] // slots]
        return carry

    lax.fori_loop(0, slots, take, 0)
    every_other(lambda other: adapter_copy(other, my_dp).wait_send())
    every_other(lambda other: grad_copy(other, my_dp).wait_send())
    for stream in streams:
        for step in range(length(stream)):
            gather(step, stream).wait_send()
            small(step, stream).wait_send()
            sum_copy(step + hops - length(stream), stream).wait_send()


def finish_kernel(
    val_ref,
    tg_ref,
    grad_ref,
    ad_ref,
    au_ref,
    df_ref,
    ds_ref,
    uf_ref,
    us_ref,
    val_out,
    tg_out,
    nd_ref,
    ndf_ref,
    nds_ref,
    nu_ref,
    nuf_ref,
    nus_ref,
):
    width = ad_ref.shape[2]
    val_out[...] = val_ref[...]
    tg_out[...] = tg_ref[...]
    for j in range(ad_ref.shape[0]):
        nd_ref[j], ndf_ref[j], nds_ref[j] = adam_update(
            ad_ref[j], df_ref[j], ds_ref[j], grad_ref[j, :, :width]
        )
        nu_ref[j], nuf_ref[j], nus_ref[j] = adam_update(
            au_ref[j], uf_ref[j], us_ref[j], grad_ref[j, :, width:]
        )


def per_device(
    tokens,
    weight,
    cotangent,
    slot_job,
    slot_count,
    adapter_down,
    adapter_up,
    down_first,
    down_second,
    up_first,
    up_second,
):
    n_dp = lax.axis_size("dp")
    n_z = lax.axis_size("tensor")
    slots, rank, width = adapter_down.shape
    cols = adapter_up.shape[2]
    rows = tokens.shape[0]
    group = lax.axis_index("dp")
    groups = jnp.arange(n_dp, dtype=jnp.int32)
    local = jnp.arange(slots, dtype=jnp.int32)
    my_jobs = lax.dynamic_slice_in_dim(slot_job, group * slots, slots)
    to_owner = jnp.sum(
        jnp.where((my_jobs // slots)[None, :] == groups[:, None], local[None, :], 0), axis=1
    )
    match = slot_job[None, :] == (group * slots + local)[:, None]
    all_slots = jnp.arange(slot_job.shape[0], dtype=jnp.int32)
    job_place = jnp.sum(jnp.where(match, all_slots[None, :], 0), axis=1)
    to_group = jnp.sum(
        jnp.where((job_place // slots)[None, :] == groups[:, None], local[None, :], 0), axis=1
    )

    smem = pl.BlockSpec(memory_space=pltpu.SMEM)
    vmem = pl.BlockSpec(memory_space=pltpu.VMEM)
    whole = pl.BlockSpec(memory_space=pl.ANY)
    hops = n_z // 2
    f32, bf16 = jnp.float32, jnp.bfloat16
    dma = pltpu.SemaphoreType.DMA
    shape = jax.ShapeDtypeStruct
    both = width + cols
    coded = (4, hops, rows // 2 + code_rows, cols)
    values, token_grad, grads = pl.pallas_call(
        functools.partial(step_kernel, n_dp, n_z),
        out_shape=(
            shape(cotangent.shape, bf16),
            shape(tokens.shape, bf16),
            shape((slots, rank, both), f32),
        ),
        in_specs=[smem] * 5 + [whole] * 2 + [vmem] * 3,
        out_specs=(vmem,) * 3,
        scratch_shapes=[
            pltpu.VMEM(tokens.shape, bf16),
            pltpu.VMEM(weight.shape, bf16),
            pltpu.VMEM((n_dp, rank, both), bf16),
            pltpu.VMEM((n_dp, rank, both), bf16),
            pltpu.VMEM((n_dp, rank, both), f32),
            pltpu.VMEM((n_dp, rank, both), f32),
            pltpu.VMEM((slots * rank, both), f32),
            pltpu.VMEM((slots, rank, both), f32),
            pltpu.VMEM((n_z, rows, cols), bf16),
            pltpu.VMEM((n_z, 2 * rank, rows), f32),
            pltpu.VMEM((n_z, rows, cols), f32),
            pltpu.VMEM(coded, jnp.int16),
            pltpu.VMEM(coded, jnp.int16),
            pltpu.VMEM((rows, width), f32),
            dma((2,)),
        ]
        + [dma((n_dp,))] * 4
        + [dma((4, hops))] * 6,
        compiler_params=pltpu.CompilerParams(collective_id=0, has_side_effects=True),
        name="adapter_step",
    )(
        slot_job,
        slot_count,
        to_group,
        to_owner,
        job_place,
        tokens,
        weight,
        cotangent,
        adapter_down,
        adapter_up,
    )
    down = shape(adapter_down.shape, f32)
    up = shape(adapter_up.shape, f32)
    return pl.pallas_call(
        finish_kernel,
        out_shape=(
            shape(values.shape, bf16),
            shape(token_grad.shape, bf16),
            down,
            down,
            down,
            up,
            up,
            up,
        ),
        in_specs=[vmem] * 9,
        out_specs=(vmem,) * 8,
        name="finish",
    )(
        values,
        token_grad,
        grads,
        adapter_down,
        adapter_up,
        down_first,
        down_second,
        up_first,
        up_second,
    )


def solution(mesh):
    in_specs = (
        P("dp", "tensor"),
        P("tensor", None),
        P("dp", "tensor"),
        P(),
        P("dp"),
        P("dp", None, "tensor"),
        P("dp", None, "tensor"),
        P("dp", None, "tensor"),
        P("dp", None, "tensor"),
        P("dp", None, "tensor"),
        P("dp", None, "tensor"),
    )
    out_specs = (
        P("dp", "tensor"),
        P("dp", "tensor"),
        P("dp", None, "tensor"),
        P("dp", None, "tensor"),
        P("dp", None, "tensor"),
        P("dp", None, "tensor"),
        P("dp", None, "tensor"),
        P("dp", None, "tensor"),
    )
    return jax.shard_map(
        per_device, mesh=mesh, in_specs=in_specs, out_specs=out_specs, check_vma=False
    )
```

```python
import functools

import jax
import jax.numpy as jnp
from jax import lax
from jax.experimental import pallas as pl
from jax.experimental.pallas import tpu as pltpu
from jax.sharding import PartitionSpec as P

lowrank_scale = 2.0
learn_rate = 0.001
beta_first = 0.9
beta_second = 0.999
adam_eps = 1e-08
adam_step = 20.0
begin_at = 1
middle_at = 3
end_at = 5
sum_lag = 0
ln2 = 0.6931471805599453
inv_ln2 = 1.4426950408889634
code_bits = 14.0
code_rows = 16
MESH = pl.DeviceIdType.MESH


def adam_update(param, first, second, grad):
    new_first = beta_first * first + (1.0 - beta_first) * grad
    new_second = beta_second * second + (1.0 - beta_second) * grad * grad
    fix_first = 1.0 - beta_first**adam_step
    fix_second = 1.0 - beta_second**adam_step
    new_param = param - learn_rate * (new_first / fix_first) / (
        jnp.sqrt(new_second / fix_second) + adam_eps
    )
    return (new_param, new_first, new_second)


def dot(a, b, dims):
    return lax.dot_general(a, b, (dims, ((), ())), preferred_element_type=jnp.float32)


def dot_split(a, b, dims):
    high = a.astype(jnp.bfloat16)
    rest = (a - high.astype(jnp.float32)).astype(jnp.bfloat16)
    return dot(high, b, dims) + dot(rest, b, dims)


def encode(x, rows):
    top = jnp.max(jnp.abs(x), axis=0, keepdims=True)
    power = jnp.ceil(jnp.log(jnp.maximum(top, 1e-28)) * inv_ln2)
    fixed = jnp.round(x * jnp.exp((code_bits - power) * ln2)).astype(jnp.int32)
    tail = jnp.broadcast_to(power, (code_rows, x.shape[1])).astype(jnp.int32)
    return fixed.astype(jnp.int16), tail.astype(jnp.int16)


def decode(ref, rows):
    power = ref[rows:, :].astype(jnp.int32).astype(jnp.float32)[:1]
    return ref[:rows, :].astype(jnp.int32).astype(jnp.float32) * jnp.exp(
        (power - code_bits) * ln2
    )


def step_kernel(
    n_dp,
    n_z,
    job_ref,
    count_ref,
    to_group_ref,
    to_owner_ref,
    group_ref,
    tok_hbm,
    w_hbm,
    cot_ref,
    ad_ref,
    au_ref,
    val_ref,
    tg_ref,
    grad_ref,
    tok_ref,
    w_ref,
    send_a,
    recv_a,
    send_g,
    recv_g,
    slot_a,
    slot_g,
    ag,
    sm_part,
    sm_in,
    sm_own,
    sm_all,
    part,
    sum_out,
    sum_in,
    back,
    load_sem,
    sem_as,
    sem_ar,
    sem_gs,
    sem_gr,
    ag_s,
    ag_r,
    rs_s,
    rs_r,
    sm_ps,
    sm_pr,
    sm_ts,
    sm_tr,
):
    my_dp = lax.axis_index("dp")
    me = lax.axis_index("tensor")
    right = lax.rem(me + 1, n_z)
    left = lax.rem(me + n_z - 1, n_z)
    hops = n_z // 2
    slots, rank, width = ad_ref.shape
    cols = cot_ref.shape[1]
    rows = cot_ref.shape[0]
    half = rows // 2
    block = rows // slots

    load_w = pltpu.make_async_copy(w_hbm, w_ref, load_sem.at[0])
    load_tok = pltpu.make_async_copy(tok_hbm, tok_ref, load_sem.at[1])
    load_tok.start()
    load_w.start()

    barrier = pltpu.get_barrier_semaphore()
    def greet(i, carry):
        other = lax.rem(my_dp + i, n_dp)
        pl.semaphore_signal(barrier, inc=1, device_id={"dp": other}, device_id_type=MESH)
        return carry

    def greet_z(i, carry):
        other = lax.rem(me + i, n_z)
        pl.semaphore_signal(barrier, inc=1, device_id={"tensor": other}, device_id_type=MESH)
        return carry

    lax.fori_loop(1, n_z, greet_z, 0)
    lax.fori_loop(1, n_dp, greet, 0)

    at_row = lax.broadcasted_iota(jnp.int32, (block, cols), 0)
    for b in range(slots):
        here = pl.ds(b * block, block)
        ag[me, here, :] = jnp.where(
            at_row < count_ref[b], cot_ref[here, :].astype(jnp.float32), 0.0
        ).astype(jnp.bfloat16)

    def pack(g, carry):
        j = to_group_ref[g]
        send_a[g, :, :width] = ad_ref[j].astype(jnp.bfloat16)
        send_a[g, :, width:] = au_ref[j].astype(jnp.bfloat16)
        return carry

    lax.fori_loop(0, n_dp, pack, 0)
    pl.semaphore_wait(barrier, n_dp + n_z - 2)

    def adapter_copy(other, slot):
        return pltpu.make_async_remote_copy(
            src_ref=send_a.at[other],
            dst_ref=recv_a.at[slot],
            send_sem=sem_as.at[other],
            recv_sem=sem_ar.at[slot],
            device_id={"dp": other},
            device_id_type=MESH,
        )

    def grad_copy(other, slot):
        return pltpu.make_async_remote_copy(
            src_ref=send_g.at[other],
            dst_ref=recv_g.at[slot],
            send_sem=sem_gs.at[other],
            recv_sem=sem_gr.at[slot],
            device_id={"dp": other},
            device_id_type=MESH,
        )

    def every_other(action):
        def body(i, carry):
            action(lax.rem(my_dp + i, n_dp))
            return carry

        lax.fori_loop(1, n_dp, body, 0)

    streams = [(0, True), (1, False), (0, False), (1, True)]

    def length(stream):
        h, to_right = stream
        return hops if (h == 0) == to_right else hops - 1

    def index(stream):
        return stream[0] * 2 + int(stream[1])

    def ring_copy(buf, size, sems, stream, step, arriving):
        h, to_right = stream
        back_by = step + 1 if arriving else step
        owner = lax.rem(me + (2 * n_z - back_by if to_right else back_by), n_z)
        place = buf.at[owner, pl.ds(h * size, size), :]
        return pltpu.make_async_remote_copy(
            src_ref=place,
            dst_ref=place,
            send_sem=sems[0].at[index(stream), step],
            recv_sem=sems[1].at[index(stream), step],
            device_id={"tensor": right if to_right else left},
            device_id_type=MESH,
        )

    def gather(step, stream, arriving=False):
        return ring_copy(ag, half, (ag_s, ag_r), stream, step, arriving)

    per = sm_own.shape[0]

    def rank_part(other, slot):
        return pltpu.make_async_remote_copy(
            src_ref=sm_part.at[other],
            dst_ref=sm_in.at[slot],
            send_sem=sm_ps.at[other],
            recv_sem=sm_pr.at[slot],
            device_id={"tensor": other},
            device_id_type=MESH,
        )

    def rank_sum(other, slot):
        return pltpu.make_async_remote_copy(
            src_ref=sm_own,
            dst_ref=sm_all.at[slot],
            send_sem=sm_ts.at[other],
            recv_sem=sm_tr.at[slot],
            device_id={"tensor": other},
            device_id_type=MESH,
        )

    def every_z(action):
        def body(i, carry):
            action(lax.rem(me + i, n_z))
            return carry

        lax.fori_loop(1, n_z, body, 0)

    def relay(ring, step):
        for stream in streams:
            if step < length(stream):
                ring(step, stream, True).wait_recv()
                if step + 1 < length(stream):
                    ring(step + 1, stream).start()

    def sum_copy(step, stream):
        i = index(stream)
        return pltpu.make_async_remote_copy(
            src_ref=sum_out.at[i, step],
            dst_ref=sum_in.at[i, step],
            send_sem=rs_s.at[i, step],
            recv_sem=rs_r.at[i, step],
            device_id={"tensor": right if stream[1] else left},
            device_id_type=MESH,
        )

    def columns(c):
        return pl.ds(pl.multiple_of(c * cols, cols), cols)

    def chunk(offset):
        return lax.rem(me + n_z + offset, n_z)

    def forward(offsets):
        w = [w_ref[:, columns(chunk(o))] for o in offsets]
        w = w[0] if len(w) == 1 else jnp.concatenate(w, axis=1)
        product = dot(tok_ref[...], w, ((1,), (0,)))
        for i, o in enumerate(offsets):
            part[chunk(o)] = product[:, i * cols : (i + 1) * cols]

    def forward_for(step):
        ahead = hops - step
        forward([ahead, -ahead] if 0 < ahead < hops else [ahead])

    def backward(offsets, first=False):
        cot = [ag[chunk(o)] for o in offsets]
        w = [w_ref[:, columns(chunk(o))] for o in offsets]
        cot = cot[0] if len(cot) == 1 else jnp.concatenate(cot, axis=1)
        w = w[0] if len(w) == 1 else jnp.concatenate(w, axis=1)
        term = dot(cot, w, ((1,), (1,)))
        back[...] = term if first else back[...] + term

    def sum_step(step):
        for stream in streams:
            start = hops - length(stream)
            if step < start:
                continue
            h, to_right = stream
            i = index(stream)
            here = pl.ds(h * half, half)
            ahead = hops - step
            c = chunk(ahead if to_right else -ahead)
            total = part[c, here, :]
            if step > start:
                sum_copy(step - 1, stream).wait_recv()
                total = total + decode(sum_in.at[i, step - 1], half)
            if step == hops:
                part[c, here, :] = total
                continue
            sum_out[i, step, :half, :], sum_out[i, step, half:, :] = encode(total, half)
            sum_copy(step, stream).start()

    of_slot = lax.broadcasted_iota(jnp.int32, (slots, rank, rows), 2) // block
    own_slot = of_slot == lax.broadcasted_iota(jnp.int32, (slots, rank, rows), 0)

    def fold(full):
        return jnp.sum(jnp.where(own_slot, full.reshape(slots, rank, rows), 0.0), axis=0)

    def unfold(ranks):
        return jnp.where(own_slot, ranks[None], 0.0).reshape(slots * rank, rows)

    def small_begin():
        every_other(lambda other: adapter_copy(my_dp, other).wait_recv())
        for b in range(slots):
            owner = job_ref[my_dp * slots + b] // slots
            slot_a[b * rank : (b + 1) * rank, :] = recv_a[owner].astype(jnp.float32)
        own = slot_a[...].astype(jnp.bfloat16)
        low = fold(dot(own[:, :width], tok_ref[...], ((1,), (1,))))
        up = fold(dot(own[:, width:], ag[me], ((1,), (1,))))
        for r in range(n_z):
            at = r * per % rank
            sm_part[r] = (low if r * per < rank else up)[at : at + per]
        every_z(lambda other: rank_part(other, me).start())
        sm_in[me] = sm_part[me]

    def small_middle():
        every_z(lambda other: rank_part(me, other).wait_recv())
        total = sm_in[0]
        for c in range(1, n_z):
            total = total + sm_in[c]
        sm_own[...] = total
        every_z(lambda other: rank_sum(other, me).start())
        sm_all[me] = total

    def small_end():
        every_z(lambda other: rank_sum(me, other).wait_recv())
        per_half = n_z // 2
        low = unfold(jnp.concatenate([sm_all[r] for r in range(per_half)], axis=0))
        up = unfold(jnp.concatenate([sm_all[r] for r in range(per_half, n_z)], axis=0))
        grads = (
            dot_split(up, tok_ref[...], ((1,), (0,))),
            dot_split(low, ag[me], ((1,), (0,))),
        )
        for b in range(slots):
            count = jnp.full((rank, cols), count_ref[b], jnp.int32).astype(jnp.float32)
            factor = (lowrank_scale / count)[:, :1]
            for grad, at in zip(grads, (pl.ds(0, width), pl.ds(width, cols))):
                slot_g[b, :, at] = factor * grad[b * rank : (b + 1) * rank]

        def pack_grad(g, carry):
            send_g[g] = slot_g[to_owner_ref[g]]
            return carry

        lax.fori_loop(0, n_dp, pack_grad, 0)
        every_other(lambda other: grad_copy(other, my_dp).start())
        recv_g[my_dp] = send_g[my_dp]
        return low, up

    def back_branch(up):
        own = slot_a[:, :width].astype(jnp.bfloat16)
        back[...] += lowrank_scale * dot_split(up, own, ((0,), (0,)))

    def value_branch(low):
        own = slot_a[:, width:].astype(jnp.bfloat16)
        part[me] += lowrank_scale * dot_split(low, own, ((0,), (0,)))

    for stream in streams:
        gather(0, stream).start()
    every_other(lambda other: adapter_copy(other, my_dp).start())
    recv_a[my_dp] = send_a[my_dp]
    load_tok.wait()
    load_w.wait()
    forward_for(0)
    backward([0], True)

    for t in range(hops + sum_lag + 1):
        u = t - sum_lag
        if 0 <= u <= hops:
            sum_step(u)
        if t < hops:
            relay(gather, t)
        if t == begin_at:
            small_begin()
        if t == middle_at:
            small_middle()
        if t == end_at:
            low, up = small_end()
        if t < hops:
            backward([-1 - t, 1 + t] if t + 1 < hops else [hops])
            forward_for(t + 1)
        if t == end_at + 1:
            back_branch(up)
        if t == hops - 1:
            value_branch(low)
            tg_ref[...] = back[...].astype(jnp.bfloat16)

    val_ref[...] = part[me].astype(jnp.bfloat16)
    every_other(lambda other: grad_copy(my_dp, other).wait_recv())

    def take(j, carry):
        grad_ref[j] = recv_g[group_ref[j] // slots]
        return carry

    lax.fori_loop(0, slots, take, 0)
    every_other(lambda other: adapter_copy(other, my_dp).wait_send())
    every_other(lambda other: grad_copy(other, my_dp).wait_send())
    every_z(lambda other: rank_part(other, me).wait_send())
    every_z(lambda other: rank_sum(other, me).wait_send())
    for stream in streams:
        for step in range(length(stream)):
            gather(step, stream).wait_send()
            sum_copy(step + hops - length(stream), stream).wait_send()


def finish_kernel(
    val_ref,
    tg_ref,
    grad_ref,
    ad_ref,
    au_ref,
    df_ref,
    ds_ref,
    uf_ref,
    us_ref,
    val_out,
    tg_out,
    nd_ref,
    ndf_ref,
    nds_ref,
    nu_ref,
    nuf_ref,
    nus_ref,
):
    width = ad_ref.shape[2]
    val_out[...] = val_ref[...]
    tg_out[...] = tg_ref[...]
    for j in range(ad_ref.shape[0]):
        nd_ref[j], ndf_ref[j], nds_ref[j] = adam_update(
            ad_ref[j], df_ref[j], ds_ref[j], grad_ref[j, :, :width]
        )
        nu_ref[j], nuf_ref[j], nus_ref[j] = adam_update(
            au_ref[j], uf_ref[j], us_ref[j], grad_ref[j, :, width:]
        )


def per_device(
    tokens,
    weight,
    cotangent,
    slot_job,
    slot_count,
    adapter_down,
    adapter_up,
    down_first,
    down_second,
    up_first,
    up_second,
):
    n_dp = lax.axis_size("dp")
    n_z = lax.axis_size("tensor")
    slots, rank, width = adapter_down.shape
    cols = adapter_up.shape[2]
    rows = tokens.shape[0]
    group = lax.axis_index("dp")
    groups = jnp.arange(n_dp, dtype=jnp.int32)
    local = jnp.arange(slots, dtype=jnp.int32)
    my_jobs = lax.dynamic_slice_in_dim(slot_job, group * slots, slots)
    to_owner = jnp.sum(
        jnp.where((my_jobs // slots)[None, :] == groups[:, None], local[None, :], 0), axis=1
    )
    match = slot_job[None, :] == (group * slots + local)[:, None]
    all_slots = jnp.arange(slot_job.shape[0], dtype=jnp.int32)
    job_place = jnp.sum(jnp.where(match, all_slots[None, :], 0), axis=1)
    to_group = jnp.sum(
        jnp.where((job_place // slots)[None, :] == groups[:, None], local[None, :], 0), axis=1
    )

    smem = pl.BlockSpec(memory_space=pltpu.SMEM)
    vmem = pl.BlockSpec(memory_space=pltpu.VMEM)
    whole = pl.BlockSpec(memory_space=pl.ANY)
    hops = n_z // 2
    per = 2 * rank // n_z
    f32, bf16 = jnp.float32, jnp.bfloat16
    dma = pltpu.SemaphoreType.DMA
    shape = jax.ShapeDtypeStruct
    both = width + cols
    coded = (4, hops, rows // 2 + code_rows, cols)
    values, token_grad, grads = pl.pallas_call(
        functools.partial(step_kernel, n_dp, n_z),
        out_shape=(
            shape(cotangent.shape, bf16),
            shape(tokens.shape, bf16),
            shape((slots, rank, both), f32),
        ),
        in_specs=[smem] * 5 + [whole] * 2 + [vmem] * 3,
        out_specs=(vmem,) * 3,
        scratch_shapes=[
            pltpu.VMEM(tokens.shape, bf16),
            pltpu.VMEM(weight.shape, bf16),
            pltpu.VMEM((n_dp, rank, both), bf16),
            pltpu.VMEM((n_dp, rank, both), bf16),
            pltpu.VMEM((n_dp, rank, both), f32),
            pltpu.VMEM((n_dp, rank, both), f32),
            pltpu.VMEM((slots * rank, both), f32),
            pltpu.VMEM((slots, rank, both), f32),
            pltpu.VMEM((n_z, rows, cols), bf16),
            pltpu.VMEM((n_z, per, rows), f32),
            pltpu.VMEM((n_z, per, rows), f32),
            pltpu.VMEM((per, rows), f32),
            pltpu.VMEM((n_z, per, rows), f32),
            pltpu.VMEM((n_z, rows, cols), f32),
            pltpu.VMEM(coded, jnp.int16),
            pltpu.VMEM(coded, jnp.int16),
            pltpu.VMEM((rows, width), f32),
            dma((2,)),
        ]
        + [dma((n_dp,))] * 4
        + [dma((4, hops))] * 4
        + [dma((n_z,))] * 4,
        compiler_params=pltpu.CompilerParams(collective_id=0, has_side_effects=True),
        name="adapter_step",
    )(
        slot_job,
        slot_count,
        to_group,
        to_owner,
        job_place,
        tokens,
        weight,
        cotangent,
        adapter_down,
        adapter_up,
    )
    down = shape(adapter_down.shape, f32)
    up = shape(adapter_up.shape, f32)
    return pl.pallas_call(
        finish_kernel,
        out_shape=(
            shape(values.shape, bf16),
            shape(token_grad.shape, bf16),
            down,
            down,
            down,
            up,
            up,
            up,
        ),
        in_specs=[vmem] * 9,
        out_specs=(vmem,) * 8,
        name="finish",
    )(
        values,
        token_grad,
        grads,
        adapter_down,
        adapter_up,
        down_first,
        down_second,
        up_first,
        up_second,
    )


def solution(mesh):
    in_specs = (
        P("dp", "tensor"),
        P("tensor", None),
        P("dp", "tensor"),
        P(),
        P("dp"),
        P("dp", None, "tensor"),
        P("dp", None, "tensor"),
        P("dp", None, "tensor"),
        P("dp", None, "tensor"),
        P("dp", None, "tensor"),
        P("dp", None, "tensor"),
    )
    out_specs = (
        P("dp", "tensor"),
        P("dp", "tensor"),
        P("dp", None, "tensor"),
        P("dp", None, "tensor"),
        P("dp", None, "tensor"),
        P("dp", None, "tensor"),
        P("dp", None, "tensor"),
        P("dp", None, "tensor"),
    )
    return jax.shard_map(
        per_device, mesh=mesh, in_specs=in_specs, out_specs=out_specs, check_vma=False
    )
```

```python
import functools

import jax
import jax.numpy as jnp
from jax import lax
from jax.experimental import pallas as pl
from jax.experimental.pallas import tpu as pltpu
from jax.sharding import PartitionSpec as P

lowrank_scale = 2.0
learn_rate = 0.001
beta_first = 0.9
beta_second = 0.999
adam_eps = 1e-08
adam_step = 20.0
begin_at = 2
middle_at = 4
end_at = 6
sum_lag = 0
ln2 = 0.6931471805599453
inv_ln2 = 1.4426950408889634
code_bits = 14.0
code_rows = 16
MESH = pl.DeviceIdType.MESH


def adam_update(param, first, second, grad):
    new_first = beta_first * first + (1.0 - beta_first) * grad
    new_second = beta_second * second + (1.0 - beta_second) * grad * grad
    fix_first = 1.0 - beta_first**adam_step
    fix_second = 1.0 - beta_second**adam_step
    new_param = param - learn_rate * (new_first / fix_first) / (
        jnp.sqrt(new_second / fix_second) + adam_eps
    )
    return (new_param, new_first, new_second)


def dot(a, b, dims):
    return lax.dot_general(a, b, (dims, ((), ())), preferred_element_type=jnp.float32)


def dot_split(a, b, dims):
    high = a.astype(jnp.bfloat16)
    rest = (a - high.astype(jnp.float32)).astype(jnp.bfloat16)
    return dot(high, b, dims) + dot(rest, b, dims)


def encode(x, rows):
    top = jnp.max(jnp.abs(x), axis=0, keepdims=True)
    power = jnp.ceil(jnp.log(jnp.maximum(top, 1e-28)) * inv_ln2)
    fixed = jnp.round(x * jnp.exp((code_bits - power) * ln2)).astype(jnp.int32)
    tail = jnp.broadcast_to(power, (code_rows, x.shape[1])).astype(jnp.int32)
    return fixed.astype(jnp.int16), tail.astype(jnp.int16)


def decode(ref, rows):
    power = ref[rows:, :].astype(jnp.int32).astype(jnp.float32)[:1]
    return ref[:rows, :].astype(jnp.int32).astype(jnp.float32) * jnp.exp(
        (power - code_bits) * ln2
    )


def step_kernel(
    n_dp,
    n_z,
    job_ref,
    count_ref,
    to_group_ref,
    to_owner_ref,
    group_ref,
    tok_hbm,
    w_hbm,
    cot_ref,
    ad_ref,
    au_ref,
    val_ref,
    tg_ref,
    grad_ref,
    tok_ref,
    w_ref,
    send_a,
    recv_a,
    send_g,
    recv_g,
    slot_a,
    slot_g,
    ag,
    sm_part,
    sm_in,
    sm_own,
    sm_all,
    part,
    sum_out,
    sum_in,
    back,
    load_sem,
    sem_as,
    sem_ar,
    sem_gs,
    sem_gr,
    ag_s,
    ag_r,
    rs_s,
    rs_r,
    sm_ps,
    sm_pr,
    sm_ts,
    sm_tr,
):
    my_dp = lax.axis_index("dp")
    me = lax.axis_index("tensor")
    right = lax.rem(me + 1, n_z)
    left = lax.rem(me + n_z - 1, n_z)
    hops = n_z // 2
    slots, rank, width = ad_ref.shape
    cols = cot_ref.shape[1]
    rows = cot_ref.shape[0]
    half = rows // 2
    block = rows // slots

    load_w = pltpu.make_async_copy(w_hbm, w_ref, load_sem.at[0])
    load_tok = pltpu.make_async_copy(tok_hbm, tok_ref, load_sem.at[1])
    load_tok.start()
    load_w.start()

    barrier = pltpu.get_barrier_semaphore()
    def greet(i, carry):
        other = lax.rem(my_dp + i, n_dp)
        pl.semaphore_signal(barrier, inc=1, device_id={"dp": other}, device_id_type=MESH)
        return carry

    def greet_z(i, carry):
        other = lax.rem(me + i, n_z)
        pl.semaphore_signal(barrier, inc=1, device_id={"tensor": other}, device_id_type=MESH)
        return carry

    lax.fori_loop(1, n_z, greet_z, 0)
    lax.fori_loop(1, n_dp, greet, 0)

    at_row = lax.broadcasted_iota(jnp.int32, (block, cols), 0)
    for b in range(slots):
        here = pl.ds(b * block, block)
        ag[me, here, :] = jnp.where(
            at_row < count_ref[b], cot_ref[here, :].astype(jnp.float32), 0.0
        ).astype(jnp.bfloat16)

    def pack(g, carry):
        j = to_group_ref[g]
        send_a[g, :, :width] = ad_ref[j].astype(jnp.bfloat16)
        send_a[g, :, width:] = au_ref[j].astype(jnp.bfloat16)
        return carry

    lax.fori_loop(0, n_dp, pack, 0)
    pl.semaphore_wait(barrier, n_dp + n_z - 2)

    def adapter_copy(other, slot):
        return pltpu.make_async_remote_copy(
            src_ref=send_a.at[other],
            dst_ref=recv_a.at[slot],
            send_sem=sem_as.at[other],
            recv_sem=sem_ar.at[slot],
            device_id={"dp": other},
            device_id_type=MESH,
        )

    def grad_copy(other, slot):
        return pltpu.make_async_remote_copy(
            src_ref=send_g.at[other],
            dst_ref=recv_g.at[slot],
            send_sem=sem_gs.at[other],
            recv_sem=sem_gr.at[slot],
            device_id={"dp": other},
            device_id_type=MESH,
        )

    def every_other(action):
        def body(i, carry):
            action(lax.rem(my_dp + i, n_dp))
            return carry

        lax.fori_loop(1, n_dp, body, 0)

    streams = [(0, True), (1, False), (0, False), (1, True)]

    def length(stream):
        h, to_right = stream
        return hops if (h == 0) == to_right else hops - 1

    def index(stream):
        return stream[0] * 2 + int(stream[1])

    def ring_copy(buf, size, sems, stream, step, arriving):
        h, to_right = stream
        back_by = step + 1 if arriving else step
        owner = lax.rem(me + (2 * n_z - back_by if to_right else back_by), n_z)
        place = buf.at[owner, pl.ds(h * size, size), :]
        return pltpu.make_async_remote_copy(
            src_ref=place,
            dst_ref=place,
            send_sem=sems[0].at[index(stream), step],
            recv_sem=sems[1].at[index(stream), step],
            device_id={"tensor": right if to_right else left},
            device_id_type=MESH,
        )

    def gather(step, stream, arriving=False):
        return ring_copy(ag, half, (ag_s, ag_r), stream, step, arriving)

    per = sm_own.shape[0]

    def rank_part(other, slot):
        return pltpu.make_async_remote_copy(
            src_ref=sm_part.at[other],
            dst_ref=sm_in.at[slot],
            send_sem=sm_ps.at[other],
            recv_sem=sm_pr.at[slot],
            device_id={"tensor": other},
            device_id_type=MESH,
        )

    def rank_sum(other, slot):
        return pltpu.make_async_remote_copy(
            src_ref=sm_own,
            dst_ref=sm_all.at[slot],
            send_sem=sm_ts.at[other],
            recv_sem=sm_tr.at[slot],
            device_id={"tensor": other},
            device_id_type=MESH,
        )

    def every_z(action):
        def body(i, carry):
            action(lax.rem(me + i, n_z))
            return carry

        lax.fori_loop(1, n_z, body, 0)

    def relay(ring, step):
        for stream in streams:
            if step < length(stream):
                ring(step, stream, True).wait_recv()
                if step + 1 < length(stream):
                    ring(step + 1, stream).start()

    def sum_copy(step, stream):
        i = index(stream)
        return pltpu.make_async_remote_copy(
            src_ref=sum_out.at[i, step],
            dst_ref=sum_in.at[i, step],
            send_sem=rs_s.at[i, step],
            recv_sem=rs_r.at[i, step],
            device_id={"tensor": right if stream[1] else left},
            device_id_type=MESH,
        )

    def columns(c):
        return pl.ds(pl.multiple_of(c * cols, cols), cols)

    def chunk(offset):
        return lax.rem(me + n_z + offset, n_z)

    def forward(offsets):
        w = [w_ref[:, columns(chunk(o))] for o in offsets]
        w = w[0] if len(w) == 1 else jnp.concatenate(w, axis=1)
        product = dot(tok_ref[...], w, ((1,), (0,)))
        for i, o in enumerate(offsets):
            part[chunk(o)] = product[:, i * cols : (i + 1) * cols]

    def forward_for(step):
        ahead = hops - step
        forward([ahead, -ahead] if 0 < ahead < hops else [ahead])

    def backward(offsets, first=False):
        cot = [ag[chunk(o)] for o in offsets]
        w = [w_ref[:, columns(chunk(o))] for o in offsets]
        cot = cot[0] if len(cot) == 1 else jnp.concatenate(cot, axis=1)
        w = w[0] if len(w) == 1 else jnp.concatenate(w, axis=1)
        term = dot(cot, w, ((1,), (1,)))
        back[...] = term if first else back[...] + term

    def sum_step(step):
        for stream in streams:
            start = hops - length(stream)
            if step < start:
                continue
            h, to_right = stream
            i = index(stream)
            here = pl.ds(h * half, half)
            ahead = hops - step
            c = chunk(ahead if to_right else -ahead)
            total = part[c, here, :]
            if step > start:
                sum_copy(step - 1, stream).wait_recv()
                total = total + decode(sum_in.at[i, step - 1], half)
            if step == hops:
                part[c, here, :] = total
                continue
            sum_out[i, step, :half, :], sum_out[i, step, half:, :] = encode(total, half)
            sum_copy(step, stream).start()

    of_slot = lax.broadcasted_iota(jnp.int32, (slots, rank, rows), 2) // block
    own_slot = of_slot == lax.broadcasted_iota(jnp.int32, (slots, rank, rows), 0)

    def fold(full):
        return jnp.sum(jnp.where(own_slot, full.reshape(slots, rank, rows), 0.0), axis=0)

    def unfold(ranks):
        return jnp.where(own_slot, ranks[None], 0.0).reshape(slots * rank, rows)

    def small_begin():
        every_other(lambda other: adapter_copy(my_dp, other).wait_recv())
        for b in range(slots):
            owner = job_ref[my_dp * slots + b] // slots
            slot_a[b * rank : (b + 1) * rank, :] = recv_a[owner].astype(jnp.float32)
        own = slot_a[...].astype(jnp.bfloat16)
        low = fold(dot(own[:, :width], tok_ref[...], ((1,), (1,))))
        up = fold(dot(own[:, width:], ag[me], ((1,), (1,))))
        for r in range(n_z):
            at = r * per % rank
            sm_part[r] = (low if r * per < rank else up)[at : at + per]
        every_z(lambda other: rank_part(other, me).start())
        sm_in[me] = sm_part[me]

    def small_middle():
        every_z(lambda other: rank_part(me, other).wait_recv())
        total = sm_in[0]
        for c in range(1, n_z):
            total = total + sm_in[c]
        sm_own[...] = total
        every_z(lambda other: rank_sum(other, me).start())
        sm_all[me] = total

    def small_end():
        every_z(lambda other: rank_sum(me, other).wait_recv())
        per_half = n_z // 2
        low = unfold(jnp.concatenate([sm_all[r] for r in range(per_half)], axis=0))
        up = unfold(jnp.concatenate([sm_all[r] for r in range(per_half, n_z)], axis=0))
        grads = (
            dot_split(up, tok_ref[...], ((1,), (0,))),
            dot_split(low, ag[me], ((1,), (0,))),
        )
        for b in range(slots):
            count = jnp.full((rank, cols), count_ref[b], jnp.int32).astype(jnp.float32)
            factor = (lowrank_scale / count)[:, :1]
            for grad, at in zip(grads, (pl.ds(0, width), pl.ds(width, cols))):
                slot_g[b, :, at] = factor * grad[b * rank : (b + 1) * rank]

        def pack_grad(g, carry):
            send_g[g] = slot_g[to_owner_ref[g]]
            return carry

        lax.fori_loop(0, n_dp, pack_grad, 0)
        every_other(lambda other: grad_copy(other, my_dp).start())
        recv_g[my_dp] = send_g[my_dp]
        return low, up

    def back_branch(up):
        own = slot_a[:, :width].astype(jnp.bfloat16)
        back[...] += lowrank_scale * dot_split(up, own, ((0,), (0,)))

    def value_branch(low):
        own = slot_a[:, width:].astype(jnp.bfloat16)
        part[me] += lowrank_scale * dot_split(low, own, ((0,), (0,)))

    for stream in streams:
        gather(0, stream).start()
    every_other(lambda other: adapter_copy(other, my_dp).start())
    recv_a[my_dp] = send_a[my_dp]
    load_tok.wait()
    load_w.wait()
    forward_for(0)
    backward([0], True)

    for t in range(hops + sum_lag + 1):
        u = t - sum_lag
        if 0 <= u <= hops:
            sum_step(u)
        if t < hops:
            relay(gather, t)
        if t == begin_at:
            small_begin()
        if t == middle_at:
            small_middle()
        if t == end_at:
            low, up = small_end()
        if t < hops:
            backward([-1 - t, 1 + t] if t + 1 < hops else [hops])
            forward_for(t + 1)
        if t == end_at + 1:
            back_branch(up)
        if t == hops - 1:
            value_branch(low)
            tg_ref[...] = back[...].astype(jnp.bfloat16)

    val_ref[...] = part[me].astype(jnp.bfloat16)
    every_other(lambda other: grad_copy(my_dp, other).wait_recv())

    def take(j, carry):
        grad_ref[j] = recv_g[group_ref[j] // slots]
        return carry

    lax.fori_loop(0, slots, take, 0)
    every_other(lambda other: adapter_copy(other, my_dp).wait_send())
    every_other(lambda other: grad_copy(other, my_dp).wait_send())
    every_z(lambda other: rank_part(other, me).wait_send())
    every_z(lambda other: rank_sum(other, me).wait_send())
    for stream in streams:
        for step in range(length(stream)):
            gather(step, stream).wait_send()
            sum_copy(step + hops - length(stream), stream).wait_send()


def finish_kernel(
    val_ref,
    tg_ref,
    grad_ref,
    ad_ref,
    au_ref,
    df_ref,
    ds_ref,
    uf_ref,
    us_ref,
    val_out,
    tg_out,
    nd_ref,
    ndf_ref,
    nds_ref,
    nu_ref,
    nuf_ref,
    nus_ref,
):
    width = ad_ref.shape[2]
    val_out[...] = val_ref[...]
    tg_out[...] = tg_ref[...]
    for j in range(ad_ref.shape[0]):
        nd_ref[j], ndf_ref[j], nds_ref[j] = adam_update(
            ad_ref[j], df_ref[j], ds_ref[j], grad_ref[j, :, :width]
        )
        nu_ref[j], nuf_ref[j], nus_ref[j] = adam_update(
            au_ref[j], uf_ref[j], us_ref[j], grad_ref[j, :, width:]
        )


def per_device(
    tokens,
    weight,
    cotangent,
    slot_job,
    slot_count,
    adapter_down,
    adapter_up,
    down_first,
    down_second,
    up_first,
    up_second,
):
    n_dp = lax.axis_size("dp")
    n_z = lax.axis_size("tensor")
    slots, rank, width = adapter_down.shape
    cols = adapter_up.shape[2]
    rows = tokens.shape[0]
    group = lax.axis_index("dp")
    groups = jnp.arange(n_dp, dtype=jnp.int32)
    local = jnp.arange(slots, dtype=jnp.int32)
    my_jobs = lax.dynamic_slice_in_dim(slot_job, group * slots, slots)
    to_owner = jnp.sum(
        jnp.where((my_jobs // slots)[None, :] == groups[:, None], local[None, :], 0), axis=1
    )
    match = slot_job[None, :] == (group * slots + local)[:, None]
    all_slots = jnp.arange(slot_job.shape[0], dtype=jnp.int32)
    job_place = jnp.sum(jnp.where(match, all_slots[None, :], 0), axis=1)
    to_group = jnp.sum(
        jnp.where((job_place // slots)[None, :] == groups[:, None], local[None, :], 0), axis=1
    )

    smem = pl.BlockSpec(memory_space=pltpu.SMEM)
    vmem = pl.BlockSpec(memory_space=pltpu.VMEM)
    whole = pl.BlockSpec(memory_space=pl.ANY)
    hops = n_z // 2
    per = 2 * rank // n_z
    f32, bf16 = jnp.float32, jnp.bfloat16
    dma = pltpu.SemaphoreType.DMA
    shape = jax.ShapeDtypeStruct
    both = width + cols
    coded = (4, hops, rows // 2 + code_rows, cols)
    values, token_grad, grads = pl.pallas_call(
        functools.partial(step_kernel, n_dp, n_z),
        out_shape=(
            shape(cotangent.shape, bf16),
            shape(tokens.shape, bf16),
            shape((slots, rank, both), f32),
        ),
        in_specs=[smem] * 5 + [whole] * 2 + [vmem] * 3,
        out_specs=(vmem,) * 3,
        scratch_shapes=[
            pltpu.VMEM(tokens.shape, bf16),
            pltpu.VMEM(weight.shape, bf16),
            pltpu.VMEM((n_dp, rank, both), bf16),
            pltpu.VMEM((n_dp, rank, both), bf16),
            pltpu.VMEM((n_dp, rank, both), f32),
            pltpu.VMEM((n_dp, rank, both), f32),
            pltpu.VMEM((slots * rank, both), f32),
            pltpu.VMEM((slots, rank, both), f32),
            pltpu.VMEM((n_z, rows, cols), bf16),
            pltpu.VMEM((n_z, per, rows), f32),
            pltpu.VMEM((n_z, per, rows), f32),
            pltpu.VMEM((per, rows), f32),
            pltpu.VMEM((n_z, per, rows), f32),
            pltpu.VMEM((n_z, rows, cols), f32),
            pltpu.VMEM(coded, jnp.int16),
            pltpu.VMEM(coded, jnp.int16),
            pltpu.VMEM((rows, width), f32),
            dma((2,)),
        ]
        + [dma((n_dp,))] * 4
        + [dma((4, hops))] * 4
        + [dma((n_z,))] * 4,
        compiler_params=pltpu.CompilerParams(collective_id=0, has_side_effects=True),
        name="adapter_step",
    )(
        slot_job,
        slot_count,
        to_group,
        to_owner,
        job_place,
        tokens,
        weight,
        cotangent,
        adapter_down,
        adapter_up,
    )
    down = shape(adapter_down.shape, f32)
    up = shape(adapter_up.shape, f32)
    return pl.pallas_call(
        finish_kernel,
        out_shape=(
            shape(values.shape, bf16),
            shape(token_grad.shape, bf16),
            down,
            down,
            down,
            up,
            up,
            up,
        ),
        in_specs=[vmem] * 9,
        out_specs=(vmem,) * 8,
        name="finish",
    )(
        values,
        token_grad,
        grads,
        adapter_down,
        adapter_up,
        down_first,
        down_second,
        up_first,
        up_second,
    )


def solution(mesh):
    in_specs = (
        P("dp", "tensor"),
        P("tensor", None),
        P("dp", "tensor"),
        P(),
        P("dp"),
        P("dp", None, "tensor"),
        P("dp", None, "tensor"),
        P("dp", None, "tensor"),
        P("dp", None, "tensor"),
        P("dp", None, "tensor"),
        P("dp", None, "tensor"),
    )
    out_specs = (
        P("dp", "tensor"),
        P("dp", "tensor"),
        P("dp", None, "tensor"),
        P("dp", None, "tensor"),
        P("dp", None, "tensor"),
        P("dp", None, "tensor"),
        P("dp", None, "tensor"),
        P("dp", None, "tensor"),
    )
    return jax.shard_map(
        per_device, mesh=mesh, in_specs=in_specs, out_specs=out_specs, check_vma=False
    )
```
